32 devices in a mesh: groups: 2 (over x), dev: 8 (over z, y), sub: 2 (over core).
Axes of the slice: x: 2, y: 2, z: 4, core: 2. Of those that a mesh axis runs over, the one named last changes fastest.
Arguments:
- hidden: bfloat16 [1024, 2048], P(('groups', 'dev', 'sub')), parts along dimension 0, may hold values from -6 to 6
- lengths: int32 [32, 32], P(('groups', 'dev', 'sub')), parts along dimension 0, may hold values from 1 to 256, 4096 in all within a row
- key_cache: bfloat16 [32, 4096, 512], P(('groups', 'dev', 'sub')), parts along dimension 0, may hold values from -320 to 320
- value_cache: bfloat16 [32, 4096, 512], P(('groups', 'dev', 'sub')), parts along dimension 0, may hold values from -6 to 6
- expert_ids: int32 [1024, 8], P(('groups', 'dev', 'sub')), parts along dimension 0, may hold values from 0 to 15, all different within a row; in each aligned block of 32 rows (0 to 31, 32 to 63, ...) at most 16 rows name the same one
- gate_codes: int32 [1024, 8], P(('groups', 'dev', 'sub')), parts along dimension 0, may hold values from 1 to 1023
- expert_device: int32 [16], replicated, may hold values from 0 to 15, each once
- attention_gain: float32 [2048], replicated, may hold values from 0.1 to 1.9
- mixture_gain: float32 [2048], replicated, may hold values from 0.1 to 1.9
- query_gain: float32 [128], replicated, may hold values from 0.1 to 1.9
- key_gain: float32 [128], replicated, may hold values from 0.1 to 1.9
- project_weight: bfloat16 [2048, 5120], P(None, 'dev'), may hold values from -0.125 to 0.125
- output_weight: bfloat16 [4096, 2048], P('dev'), may hold values from -0.09375 to 0.09375
- expert_gate_up: bfloat16 [16, 2048, 1536], P(('dev', 'sub')), may hold values from -0.125 to 0.125
- expert_down: bfloat16 [16, 768, 2048], P(('dev', 'sub')), may hold values from -0.21875 to 0.21875
Outputs:
- layer_out: bfloat16 [1024, 2048], P(('groups', 'dev', 'sub')), parts along dimension 0
The draws below stay inside these ranges and needn't reach their ends.
There are 2 independent parts, one for each index of `groups`. The reference program is written for one: setup_inputs(seed, part) draws one part's arguments, and reference() takes and returns one part's arrays. A program takes and returns all parts, laid end to end along the dimension named above; an argument that names none is the same for every part. Nothing has to cross between parts.
Inputs may be any that keep to these rules, and one draw needn't show every extreme that they name: `expert_ids`: each row names 8 different experts. Among the 32 rows of one device no expert is named more than 16 times, and in some device an expert is named exactly 16 times. The 32 lengths of each device sum to 4096; the largest of them is 256. A permutation: expert e is held by the device at index expert_device[e] of the joined axes dev and sub.
All inputs are finite; a program needn't handle non-finite values.
Results may differ from the reference program's by a relative error of at most 0.015.
Values may be sent and summed in bfloat16 or wider, within the bound.
A program may use at most 128 MiB of HBM per device.

```python
import math
import jax
import jax.numpy as jnp
import numpy as np
from jax import lax

D = 2048
HEADS = 32
KVH = 4
HD = 128
FF = 768
TOP = 8
R_DEV = 32
POOL = 4096
LMOST = 256
CAP = 16
GROUP_DEVS = 16
EXPERTS = 16
ROWS = 512
QKV = 5120


def draw_key_cache(key, part):
    normal_key = jax.random.fold_in(jax.random.fold_in(key, 7), 0)
    array_shape = (GROUP_DEVS, POOL, KVH * HD)
    normal_part = jnp.clip(jax.random.normal(normal_key, array_shape, jnp.float32), -8.0, 8.0)
    return normal_part.astype(jnp.bfloat16)


def with_ends(entries, key, smallest, high):
    place = [jax.random.randint(jax.random.fold_in(key, axis), (), 0, length) for axis, length in enumerate(entries.shape)]
    longest = entries.shape.index(max(entries.shape))
    beside = place[:longest] + [(place[longest] + 1) % entries.shape[longest]] + place[longest + 1:]
    return entries.at[tuple(place)].set(smallest).at[tuple(beside)].set(high)


def block_levels(key, dims, shards, least, largest):
    def one(axis_at, blocks):
        heights = jax.random.uniform(jax.random.fold_in(jax.random.fold_in(key, 6), axis_at), (blocks,), jnp.float32, least / len(shards), largest / len(shards))
        return jnp.repeat(jnp.exp(heights), dims[axis_at] // blocks).reshape((-1,) + (1,) * (len(dims) - axis_at - 1))

    factor_of = one(*shards[0])
    for cut in shards[1:]:
        factor_of = factor_of * one(*cut)
    return factor_of


def profile(count, total, bound, lean):
    portions = [(1 << 20) // math.isqrt(grade ** lean) + 1 for grade in range(2, count + 1)]
    spare, holding = total - bound - (count - 1), [1] * (count - 1)
    while spare > 0:
        free = [i for i in range(count - 1) if holding[i] < bound]
        whole, budget = sum([portions[i] for i in free]), spare
        for i in free:
            more = min(bound - holding[i], max(1, budget * portions[i] // whole), spare)
            holding[i] = holding[i] + more
            spare = spare - more
    return np.array([bound] + holding)


def uneven(stream_key, number_of, total, bound, lean):
    if number_of == 2:
        one = jax.random.randint(stream_key, (), max(1, total - bound), min(bound, total - 1) + 1)
        return jnp.stack([one, total - one])
    sizes = jnp.asarray(profile(number_of, total, bound, lean), jnp.int32)
    couples = (number_of - 1) // 2
    donor, receiver = sizes[1:1 + 2 * couples:2], sizes[2:2 + 2 * couples:2]
    room = jnp.minimum(donor - 1, bound - receiver)
    shifted = jax.random.randint(jax.random.fold_in(stream_key, 1), (couples,), 0, 1 << 20) % (room + 1)
    sizes = sizes.at[1:1 + 2 * couples:2].set(donor - shifted).at[2:2 + 2 * couples:2].set(receiver + shifted)
    return sizes[jax.random.permutation(jax.random.fold_in(stream_key, 2), number_of)]


def shared_out(key, own, number, rows, number_of, top, reach, slope):
    order = jax.random.permutation(key, number_of)
    heavy_load, common = shares(number_of, rows * top, reach, slope, True), shares(number_of, rows * top, reach, slope, False)
    places = jnp.arange(number_of)

    def named(sizes, turn):
        used = int((sizes > 0).sum())
        fixed = max(1, used // 4)
        moved = fixed + (places - fixed + turn * (used - fixed)) % max(1, number_of - fixed)
        return jnp.zeros((number_of,), jnp.int32).at[order[jnp.where(places < fixed, places, moved)]].set(jnp.asarray(sizes, jnp.int32))

    sizes = jnp.where(number % 4 == 0, named(heavy_load, number // 4), named(common, number - number // 4 - 1))
    mixed = jax.random.permutation(jax.random.fold_in(own, 3), number_of)
    giver, taker = mixed[0:number_of // 2 * 2:2], mixed[1:number_of // 2 * 2:2]
    room = jnp.minimum(sizes[giver] - 1, reach - sizes[taker]) // 2
    room = jnp.where((giver == order[0]) | (taker == order[0]) | (sizes[taker] == 0), 0, jnp.maximum(room, 0))
    moved = jax.random.randint(jax.random.fold_in(own, 4), (number_of // 2,), 0, 1 << 20) % (room + 1)
    sizes = sizes.at[giver].add(-moved).at[taker].add(moved)
    items = jnp.searchsorted(jnp.cumsum(sizes), jnp.arange(rows * top), side="right").astype(jnp.int32)
    grid = items.reshape(top, rows).T
    grid = grid[jax.random.permutation(jax.random.fold_in(own, 1), rows)]
    turn = jax.random.randint(jax.random.fold_in(own, 2), (rows, 1), 0, top)
    return jnp.take_along_axis(grid, (jnp.arange(top)[None, :] + turn) % top, axis=1)


def shares(count, total, most, slope, full):
    weights = [(1 << 20) // math.isqrt(grade ** slope) + 1 for grade in range(1, count + 1)]
    largest = most if full else min(most, max(-(-total // count), total * weights[0] // sum(weights)))
    least = 1 if total - largest >= count - 1 else 0
    holding, spare = [largest] + [least] * (count - 1), total - largest - least * (count - 1)
    while spare > 0:
        free = [i for i in range(1, count) if holding[i] < largest] or [i for i in range(1, count) if holding[i] < most]
        whole, budget = sum([weights[i] for i in free]), spare
        for i in free:
            more = min(most - holding[i], max(1, budget * weights[i] // whole), spare)
            holding[i] = holding[i] + more
            spare = spare - more
    return np.array(holding)


def centred(key, shape, deviation, most, cuts=(), held_as=jnp.bfloat16):
    factor_of = block_levels(key, shape, cuts, -0.22, 0.18) if cuts else 1.0
    array = jax.random.normal(key, shape, jnp.float32) * deviation * factor_of
    return jnp.minimum(jnp.maximum(array, -most), most).astype(held_as)


def setup_inputs(seed: int = 0, part: int = 0) -> dict:
    streams_of = jax.random.split(jax.random.key(seed), 16)
    part_splits = jax.random.split(jax.random.fold_in(streams_of[15], part), 16)
    hidden = centred(part_splits[0], (ROWS, D), 1.0, 6.0, ((0, 16),))
    lengths = jax.vmap(lambda own: uneven(own, R_DEV, POOL, LMOST, 2))(jax.random.split(part_splits[1], GROUP_DEVS)).reshape((GROUP_DEVS, R_DEV)).astype(jnp.int32)
    key_cache = draw_key_cache(jax.random.fold_in(jax.random.fold_in(streams_of[15], part), 71), part)
    value_cache = centred(part_splits[3], (GROUP_DEVS, POOL, KVH * HD), 1.0, 6.0, ((0, 16),))
    expert_ids_keys = jax.random.split(jax.random.fold_in(part_splits[4], 1), ROWS // R_DEV)
    expert_ids_turns = jax.random.permutation(jax.random.fold_in(part_splits[4], 3), ROWS // R_DEV)
    expert_ids = jax.vmap(lambda own, number: shared_out(jax.random.fold_in(part_splits[4], 2), own, number, R_DEV, EXPERTS, TOP, CAP, 2))(expert_ids_keys, expert_ids_turns).reshape((ROWS, TOP))
    gate_codes = with_ends(jax.random.randint(part_splits[5], (ROWS, TOP), 1, 1024), jax.random.fold_in(part_splits[5], 1), 1, 1023).astype(jnp.int32)
    expert_device = jax.random.permutation(streams_of[6], EXPERTS).astype(jnp.int32)
    attention_gain = jnp.clip(1.0 + 0.18 * jax.random.normal(streams_of[7], (D,), jnp.float32), 0.1, 1.9)
    mixture_gain = jnp.clip(1.0 + 0.18 * jax.random.normal(streams_of[8], (D,), jnp.float32), 0.1, 1.9)
    query_gain = jnp.clip(1.0 + 0.18 * jax.random.normal(streams_of[9], (HD,), jnp.float32), 0.1, 1.9)
    key_gain = jnp.clip(1.0 + 0.18 * jax.random.normal(streams_of[10], (HD,), jnp.float32), 0.1, 1.9)
    project_weight = centred(streams_of[11], (D, QKV), D ** -0.5, 0.125, ((1, 8),))
    output_weight = centred(streams_of[12], (HEADS * HD, D), (HEADS * HD) ** -0.5, 0.09375, ((0, 8),))
    expert_gate_up = centred(streams_of[13], (EXPERTS, D, 2 * FF), D ** -0.5, 0.125, ((0, 16),))
    expert_down = centred(streams_of[14], (EXPERTS, FF, D), FF ** -0.5, 0.21875, ((0, 16),))
    return {"hidden": hidden, "lengths": lengths, "key_cache": key_cache, "value_cache": value_cache, "expert_ids": expert_ids, "gate_codes": gate_codes, "expert_device": expert_device, "attention_gain": attention_gain, "mixture_gain": mixture_gain, "query_gain": query_gain, "key_gain": key_gain, "project_weight": project_weight, "output_weight": output_weight, "expert_gate_up": expert_gate_up, "expert_down": expert_down}


EPSILON = 1e-06
ROPE_BASE = 1000000.0

def norm_scale(values, scale_gain):
    mean_square = lax.optimization_barrier(jnp.mean(values * values, axis=-1, keepdims=True))
    return values * lax.rsqrt(mean_square + EPSILON) * scale_gain

def rotate(values, position):
    half_width = values.shape[-1] // 2
    frequency = ROPE_BASE ** (-jnp.arange(half_width, dtype=jnp.float32) * 2.0 / values.shape[-1])
    angles = position.astype(jnp.float32)[:, None] * frequency[None, :]
    cosine = jnp.cos(angles)[:, None, :]
    sine_part = jnp.sin(angles)[:, None, :]
    first_half = values[..., :half_width]
    second_half = values[..., half_width:]
    return jnp.concatenate([first_half * cosine - second_half * sine_part, second_half * cosine + first_half * sine_part], axis=-1)

def split_heads(merged, position, query_gain, key_gain):
    row_count = merged.shape[0]
    query_cols = HEADS * HD
    key_cols = KVH * HD
    queries = merged[:, :query_cols].astype(jnp.float32).reshape(row_count, HEADS, HD)
    queries = rotate(norm_scale(queries, query_gain), position).astype(jnp.bfloat16)
    new_keys = merged[:, query_cols:query_cols + key_cols].astype(jnp.float32).reshape(row_count, KVH, HD)
    new_keys = rotate(norm_scale(new_keys, key_gain), position).astype(jnp.bfloat16)
    new_values = merged[:, query_cols + key_cols:].reshape(row_count, KVH, HD)
    return (queries, new_keys, new_values)

def attend(queries, new_keys, new_values, key_rows, value_rows, lengths):
    row_count, head_count, head_width = queries.shape
    kv_count = new_keys.shape[1]
    group_size = head_count // kv_count
    pool_size = key_rows.shape[0]
    seg_end = jnp.cumsum(lengths).astype(jnp.int32)
    seg_start = seg_end - lengths
    position = jnp.arange(pool_size, dtype=jnp.int32)
    inside = (position[None, :] >= seg_start[:, None]) & (position[None, :] < seg_end[:, None])
    grouped = queries.reshape(row_count, kv_count, group_size, head_width).astype(jnp.float32)
    keyed = key_rows.reshape(pool_size, kv_count, head_width).astype(jnp.float32)
    valued = value_rows.reshape(pool_size, kv_count, head_width).astype(jnp.float32)
    scale = 1.0 / math.sqrt(head_width)
    scores = jnp.einsum('rkgd,pkd->krgp', grouped, keyed) * scale
    own_score = jnp.einsum('rkgd,rkd->krg', grouped, new_keys.astype(jnp.float32)) * scale
    mask = inside[None, :, None, :]
    masked = jnp.where(mask, scores, -1e+30)
    peak = jnp.maximum(lax.optimization_barrier(jnp.max(masked, axis=3)), own_score)
    raised = jnp.where(mask, jnp.exp(masked - peak[..., None]), 0.0)
    own_raised = jnp.exp(own_score - peak)
    denominator = lax.optimization_barrier(jnp.sum(raised, axis=3)) + own_raised
    weights = (raised / denominator[..., None]).astype(jnp.bfloat16)
    mixed_out = jnp.einsum('krgp,pkd->rkgd', weights.astype(jnp.float32), valued)
    own_weight = jnp.transpose(own_raised / denominator, (1, 0, 2))[..., None]
    own_part = own_weight * new_values.astype(jnp.float32)[:, :, None, :]
    return (mixed_out + own_part).reshape(row_count, head_count * head_width).astype(jnp.bfloat16)

def reference(hidden, lengths, key_cache, value_cache, expert_ids, gate_codes, expert_device, attention_gain, mixture_gain, query_gain, key_gain, project_weight, output_weight, expert_gate_up, expert_down):
    row_count = hidden.shape[0]
    normed = norm_scale(hidden.astype(jnp.float32), attention_gain).astype(jnp.bfloat16)
    merged = jnp.dot(normed, project_weight, preferred_element_type=jnp.float32).astype(jnp.bfloat16)
    position = lengths.reshape(row_count)
    queries, new_keys, new_values = split_heads(merged, position, query_gain, key_gain)

    def per_block(blocks):
        return attend(blocks[0], blocks[1], blocks[2], blocks[3], blocks[4], blocks[5])
    attention = lax.map(per_block, (queries.reshape(GROUP_DEVS, R_DEV, HEADS, HD), new_keys.reshape(GROUP_DEVS, R_DEV, KVH, HD), new_values.reshape(GROUP_DEVS, R_DEV, KVH, HD), key_cache, value_cache, lengths))
    attention = attention.reshape(row_count, HEADS * HD)
    residual = hidden.astype(jnp.float32) + jnp.dot(attention, output_weight, preferred_element_type=jnp.float32)
    mixture_in = norm_scale(residual, mixture_gain).astype(jnp.bfloat16)
    share = gate_codes.astype(jnp.float32)
    share = share / lax.optimization_barrier(jnp.sum(share, axis=1, keepdims=True))
    holder = jnp.take(expert_device, expert_ids).astype(jnp.int32)
    row_limit = min(row_count, CAP * GROUP_DEVS)

    def one_slot(total, slot_index):
        hits = holder == slot_index
        weight = lax.optimization_barrier(jnp.sum(jnp.where(hits, share, 0.0), axis=1))
        chosen = jnp.any(hits, axis=1).astype(jnp.int32)
        ranking = jnp.argsort(1 - chosen, stable=True)[:row_limit].astype(jnp.int32)
        picked = jnp.take(mixture_in, ranking, axis=0)
        both_parts = jnp.dot(picked, expert_gate_up[slot_index], preferred_element_type=jnp.float32)
        units = (jax.nn.silu(both_parts[:, :FF]) * both_parts[:, FF:]).astype(jnp.bfloat16)
        expert_out = jnp.dot(units, expert_down[slot_index], preferred_element_type=jnp.float32).astype(jnp.bfloat16)
        addition = expert_out.astype(jnp.float32) * jnp.take(weight, ranking)[:, None]
        return (total.at[ranking].add(addition), None)
    routed, unused = lax.scan(one_slot, jnp.zeros((row_count, D), jnp.float32), jnp.arange(GROUP_DEVS, dtype=jnp.int32))
    return (residual + routed).astype(jnp.bfloat16)
```

```python
import functools
import math

import jax
import jax.numpy as jnp
from jax import lax
from jax.experimental import pallas as pl
from jax.experimental.pallas import tpu as pltpu
from jax.sharding import PartitionSpec as P

HEADS = 32
KVH = 4
HD = 128

EPSILON = 1e-06
ROPE_BASE = 1000000.0
MESH = pl.DeviceIdType.MESH
VMEM = pl.BlockSpec(memory_space=pltpu.VMEM)


def norm_scale(values, scale_gain):
    mean_square = jnp.mean(values * values, axis=-1, keepdims=True)
    return values * lax.rsqrt(mean_square + EPSILON) * scale_gain


def rotate(values, position):
    half_width = values.shape[-1] // 2
    frequency = ROPE_BASE ** (-jnp.arange(half_width, dtype=jnp.float32) * 2.0 / values.shape[-1])
    angles = position.astype(jnp.float32)[:, None] * frequency[None, :]
    cosine = jnp.cos(angles)[:, None, :]
    sine_part = jnp.sin(angles)[:, None, :]
    first_half = values[..., :half_width]
    second_half = values[..., half_width:]
    return jnp.concatenate(
        [
            first_half * cosine - second_half * sine_part,
            second_half * cosine + first_half * sine_part,
        ],
        axis=-1,
    )


def place_of(dev, n):
    side = lax.rem(dev, 2)
    z = lax.div(dev, 2)
    return (1 - side) * z + side * (n - 1 - z)


def dev_at(place, n):
    place = lax.rem(place + 2 * n, n)
    side = lax.div(place, n // 2)
    return (1 - side) * (2 * place) + side * (2 * (n - 1 - place) + 1)


def greet(devs, subs=()):
    barrier = pltpu.get_barrier_semaphore()
    for dev in devs:
        pl.semaphore_signal(barrier, inc=1, device_id={"dev": dev}, device_id_type=MESH)
    for sub in subs:
        pl.semaphore_signal(barrier, inc=1, device_id={"sub": sub}, device_id_type=MESH)
    pl.semaphore_wait(barrier, len(devs) + len(subs))


def reach(n, way, half):
    return n // 2 if way == half else n // 2 - 1


def ring_gather(n, x_ref, slot, send_sem, recv_sem, on_block, on_half=None):
    me = lax.axis_index("dev")
    at = place_of(me, n)
    rows = x_ref.shape[0] // 2
    sides = (dev_at(at + 1, n), dev_at(at - 1, n))
    sent = []

    def send(src, origin, way, half, hop):
        copy = pltpu.make_async_remote_copy(
            src_ref=src,
            dst_ref=slot(origin, half),
            send_sem=send_sem.at[way, half, hop],
            recv_sem=recv_sem.at[way, half, hop],
            device_id={"dev": sides[way]},
            device_id_type=MESH,
        )
        copy.start()
        sent.append(copy)

    for half in range(2):
        for way in range(2):
            if reach(n, way, half) >= 1:
                send(x_ref.at[pl.ds(half * rows, rows)], me, way, half, 0)
    on_block(0, (me,))
    for hop in range(1, n // 2 + 1):
        origins = (dev_at(at - hop, n), dev_at(at + hop, n))
        for half in range(2):
            for way in range(2):
                if hop > reach(n, way, half):
                    continue
                origin = origins[way]
                here = slot(origin, half)
                pltpu.make_async_remote_copy(
                    src_ref=here,
                    dst_ref=here,
                    send_sem=send_sem.at[way, half, hop - 1],
                    recv_sem=recv_sem.at[way, half, hop - 1],
                    device_id={"dev": sides[way]},
                    device_id_type=MESH,
                ).wait_recv()
                if hop < reach(n, way, half):
                    send(here, origin, way, half, hop)
                if on_half is not None:
                    on_half(origin, half)
        on_block(hop, origins[:1] if 2 * hop == n else origins)
    return sent


def ring_reduce(n, part, rows, here, there, send_sem, recv_sem, out_ref):
    at = place_of(lax.axis_index("dev"), n)
    sides = (dev_at(at + 1, n), dev_at(at - 1, n))
    sent = []
    for away in range(n // 2, -1, -1):
        both = part(away, (dev_at(at + away, n), dev_at(at - away, n)))
        for half in range(2):
            total = both[0][half * rows : (half + 1) * rows] if away == 0 else None
            for way in range(2):
                far = reach(n, way, half)
                if away > far:
                    continue
                value = total if away == 0 else both[way][half * rows : (half + 1) * rows]
                if away < far:
                    pltpu.make_async_remote_copy(
                        src_ref=there.at[way, half, away],
                        dst_ref=there.at[way, half, away],
                        send_sem=send_sem.at[way, half, away],
                        recv_sem=recv_sem.at[way, half, away],
                        device_id={"dev": sides[way]},
                        device_id_type=MESH,
                    ).wait_recv()
                    value = value + there[way, half, away].astype(jnp.float32)
                if away == 0:
                    total = value
                    continue
                here[way, half, away - 1] = value.astype(here.dtype)
                copy = pltpu.make_async_remote_copy(
                    src_ref=here.at[way, half, away - 1],
                    dst_ref=there.at[way, half, away - 1],
                    send_sem=send_sem.at[way, half, away - 1],
                    recv_sem=recv_sem.at[way, half, away - 1],
                    device_id={"dev": sides[way]},
                    device_id_type=MESH,
                )
                copy.start()
                sent.append(copy)
            if away == 0:
                out_ref[half * rows : (half + 1) * rows, :] = total
    return sent


def others(n):
    me = lax.axis_index("dev")
    return [lax.rem(me + step, n) for step in range(1, n)]


def project_kernel(n, x_ref, w_ref, out_ref, held, mine, back, send_sem, recv_sem, back_send, back_recv):
    me = lax.axis_index("dev")
    at = place_of(me, n)
    rows = x_ref.shape[0]
    half_rows = rows // 2
    greet(others(n))
    waiting = []
    returned = []

    def post():
        for dev, lane in waiting:
            copy = pltpu.make_async_remote_copy(
                src_ref=mine.at[lane],
                dst_ref=back.at[lane],
                send_sem=back_send.at[lane],
                recv_sem=back_recv.at[lane],
                device_id={"dev": dev},
                device_id_type=MESH,
            )
            copy.start()
            returned.append(copy)
        waiting.clear()

    def on_block(hop, devs):
        if hop == 0:
            block = x_ref[...]
        else:
            block = jnp.concatenate([held[dev] for dev in devs], axis=0)
        product = jnp.dot(block, w_ref[...], preferred_element_type=jnp.float32).astype(mine.dtype)
        post()
        for index, dev in enumerate(devs):
            lane = hop if index == 0 else n - hop
            mine[lane] = product[index * rows : (index + 1) * rows]
            if hop > 0:
                waiting.append((dev, lane))

    sent = ring_gather(
        n,
        x_ref,
        lambda dev, half: held.at[dev, pl.ds(half * half_rows, half_rows)],
        send_sem,
        recv_sem,
        on_block,
    )
    post()
    out_ref[me] = mine[0]
    for copy in returned:
        copy.wait_recv()
    for lane in range(1, n):
        out_ref[dev_at(at + lane, n)] = back[lane]
    for copy in sent + returned:
        copy.wait_send()


def project(n, x, w, collective_id):
    rows, width = x.shape
    columns = w.shape[1]
    sems = pltpu.SemaphoreType.DMA((2, 2, n // 2))
    lanes = pltpu.SemaphoreType.DMA((n,))
    return pl.pallas_call(
        functools.partial(project_kernel, n),
        out_shape=jax.ShapeDtypeStruct((n, rows, columns), jnp.bfloat16),
        in_specs=[VMEM] * 2,
        out_specs=VMEM,
        scratch_shapes=[
            pltpu.VMEM((n, rows, width), x.dtype),
            pltpu.VMEM((n, rows, columns), jnp.bfloat16),
            pltpu.VMEM((n, rows, columns), jnp.bfloat16),
            sems,
            sems,
            lanes,
            lanes,
        ],
        compiler_params=pltpu.CompilerParams(collective_id=collective_id, has_side_effects=True),
        name="project",
    )(x, w)


def attend_kernel(tile, q_ref, nk_ref, nv_ref, first_ref, count_ref, k_ref, v_ref, out_ref, kept):
    scale = 1.0 / math.sqrt(q_ref.shape[2])
    q = q_ref[0]
    lines, width = q.shape
    requests = nk_ref.shape[1]
    fan = lines // requests

    def spread(values):
        return jnp.broadcast_to(values[:, None, :], (requests, fan, width)).reshape(lines, width)

    new_key = spread(nk_ref[0].astype(jnp.float32))
    new_value = spread(nv_ref[0].astype(jnp.float32))
    own = jnp.sum(q.astype(jnp.float32) * new_key, axis=1, keepdims=True)
    first = first_ref[...]
    last = first + count_ref[...]
    peak = own
    tiles = k_ref.shape[1] // tile
    lane = lax.broadcasted_iota(jnp.int32, (1, tile), 1)
    for index in range(tiles):
        keys = k_ref[0, index * tile : (index + 1) * tile]
        score = lax.dot_general(q, keys, (((1,), (1,)), ((), ())), preferred_element_type=jnp.float32)
        position = lane + index * tile
        inside = (position >= first) & (position < last)
        score = jnp.where(inside, score, -1e30)
        kept[index] = score
        peak = jnp.maximum(peak, jnp.max(score, axis=1, keepdims=True))
    own_raised = jnp.exp((own - peak) * scale)
    total = own_raised
    mixed = own_raised * new_value
    for index in range(tiles):
        raised = jnp.exp((kept[index] - peak) * scale)
        total = total + jnp.sum(raised, axis=1, keepdims=True)
        mixed = mixed + jnp.dot(
            raised.astype(jnp.bfloat16),
            v_ref[0, index * tile : (index + 1) * tile],
            preferred_element_type=jnp.float32,
        )
    out_ref[0] = (mixed / total).astype(out_ref.dtype)


def attend(queries, new_keys, new_values, key_cache, value_cache, lengths):
    rows, heads, width = queries.shape
    kv = new_keys.shape[1]
    fan = heads // kv
    pool = key_cache.shape[1]
    tile = math.gcd(pool, 1024)
    lines = rows * fan
    q = queries.reshape(rows, kv, fan, width).transpose(1, 0, 2, 3).reshape(kv, lines, width)
    end = jnp.cumsum(lengths)
    count = jnp.repeat(lengths, fan)[:, None]
    first = jnp.repeat(end - lengths, fan)[:, None]
    by_head = lambda *shape: pl.BlockSpec((1,) + shape, lambda head: (head, 0, 0))
    whole = pl.BlockSpec((lines, 1), lambda head: (0, 0))
    cache = pl.BlockSpec((1, pool, width), lambda head: (0, 0, head))
    out = pl.pallas_call(
        functools.partial(attend_kernel, tile),
        grid=(kv,),
        out_shape=jax.ShapeDtypeStruct((kv, lines, width), jnp.bfloat16),
        in_specs=[by_head(lines, width), by_head(rows, width), by_head(rows, width), whole, whole, cache, cache],
        out_specs=by_head(lines, width),
        scratch_shapes=[pltpu.VMEM((pool // tile, lines, tile), jnp.float32)],
        name="attend",
    )(q, new_keys.transpose(1, 0, 2), new_values.transpose(1, 0, 2), first, count, key_cache, value_cache)
    return out.reshape(kv, rows, fan, width).transpose(1, 0, 2, 3).reshape(rows, heads * width)


def output_kernel(n, a_ref, w_ref, out_ref, held, here, there, send_sem, recv_sem, move_send, move_recv):
    at = place_of(lax.axis_index("dev"), n)
    me = lax.axis_index("dev")
    rows = a_ref.shape[1]
    greet(others(n))
    moves = {}
    order = [n // 2]
    for away in range(n // 2 - 1, 0, -1):
        order += [away, n - away]
    for lane in order:
        copy = pltpu.make_async_remote_copy(
            src_ref=a_ref.at[dev_at(at - lane, n)],
            dst_ref=held.at[lane],
            send_sem=move_send.at[lane],
            recv_sem=move_recv.at[lane],
            device_id={"dev": dev_at(at - lane, n)},
            device_id_type=MESH,
        )
        copy.start()
        moves[lane] = copy

    def part(away, devs):
        lanes = (away,) if away == 0 or 2 * away == n else (away, n - away)
        if away == 0:
            features = a_ref[me]
        else:
            for lane in lanes:
                moves[lane].wait_recv()
            features = jnp.concatenate([held[lane] for lane in lanes], axis=0)
        product = jnp.dot(features, w_ref[...], preferred_element_type=jnp.float32)
        return (product[:rows], product[-rows:])

    sent = ring_reduce(n, part, rows // 2, here, there, send_sem, recv_sem, out_ref)
    for copy in sent + list(moves.values()):
        copy.wait_send()


def output(n, a, w, collective_id):
    _, rows, depth = a.shape
    width = w.shape[1]
    sems = pltpu.SemaphoreType.DMA((2, 2, n // 2))
    lanes = pltpu.SemaphoreType.DMA((n,))
    return pl.pallas_call(
        functools.partial(output_kernel, n),
        out_shape=jax.ShapeDtypeStruct((rows, width), jnp.float32),
        in_specs=[VMEM] * 2,
        out_specs=VMEM,
        scratch_shapes=[
            pltpu.VMEM((n, rows, depth), a.dtype),
            pltpu.VMEM((2, 2, n // 2, rows // 2, width), jnp.bfloat16),
            pltpu.VMEM((2, 2, n // 2, rows // 2, width), jnp.bfloat16),
            sems,
            sems,
            lanes,
            lanes,
        ],
        compiler_params=pltpu.CompilerParams(collective_id=collective_id, has_side_effects=True),
        name="output",
    )(a, w)


def gather_kernel(n, s, x_ref, out_ref, send_sem, recv_sem, pair_send, pair_recv):
    me = lax.axis_index("dev")
    at = place_of(me, n)
    sub = lax.axis_index("sub")
    rows = x_ref.shape[0] // 2
    partners = [lax.rem(sub + step, s) for step in range(1, s)]
    greet((dev_at(at + 1, n), dev_at(at - 1, n)), partners)
    pairs = []

    def share(src, origin, half):
        for step, partner in enumerate(partners):
            copy = pltpu.make_async_remote_copy(
                src_ref=src,
                dst_ref=out_ref.at[origin, sub, pl.ds(half * rows, rows)],
                send_sem=pair_send.at[step, origin, half],
                recv_sem=pair_recv.at[step, origin, half],
                device_id={"sub": partner},
                device_id_type=MESH,
            )
            copy.start()
            pairs.append((copy, step, origin, half))

    slot = lambda dev, half: out_ref.at[dev, sub, pl.ds(half * rows, rows)]

    def on_block(hop, devs):
        if hop == 0:
            for half in range(2):
                share(x_ref.at[pl.ds(half * rows, rows)], me, half)
            out_ref[me, sub] = x_ref[...]

    sent = ring_gather(
        n, x_ref, slot, send_sem, recv_sem, on_block, lambda origin, half: share(slot(origin, half), origin, half)
    )
    for copy, step, origin, half in pairs:
        came = out_ref.at[origin, lax.rem(sub + s - step - 1, s), pl.ds(half * rows, rows)]
        pltpu.make_async_remote_copy(
            src_ref=came,
            dst_ref=came,
            send_sem=pair_send.at[step, origin, half],
            recv_sem=pair_recv.at[step, origin, half],
            device_id={"sub": partners[step]},
            device_id_type=MESH,
        ).wait_recv()
    for copy in sent + [entry[0] for entry in pairs]:
        copy.wait_send()


def gather(n, s, x, collective_id):
    rows, width = x.shape
    sems = pltpu.SemaphoreType.DMA((2, 2, n // 2))
    pair = pltpu.SemaphoreType.DMA((max(s - 1, 1), n, 2))
    return pl.pallas_call(
        functools.partial(gather_kernel, n, s),
        out_shape=jax.ShapeDtypeStruct((n, s, rows, width), x.dtype),
        in_specs=[VMEM],
        out_specs=VMEM,
        scratch_shapes=[sems, sems, pair, pair],
        compiler_params=pltpu.CompilerParams(collective_id=collective_id, has_side_effects=True),
        name="gather",
    )(x)


def combine_kernel(n, s, p_ref, out_ref, near, here, there, send_sem, recv_sem, pair_send, pair_recv):
    me = lax.axis_index("dev")
    at = place_of(me, n)
    sub = lax.axis_index("sub")
    rows = p_ref.shape[2]
    partners = [lax.rem(sub + step, s) for step in range(1, s)]
    greet((dev_at(at + 1, n), dev_at(at - 1, n)), partners)
    order = [n // 2]
    for away in range(n // 2 - 1, 0, -1):
        order += [away, n - away]
    order.append(0)
    pairs = {}
    for lane in order:
        for step, partner in enumerate(partners):
            copy = pltpu.make_async_remote_copy(
                src_ref=p_ref.at[dev_at(at + lane, n), partner],
                dst_ref=near.at[step, lane],
                send_sem=pair_send.at[step, lane],
                recv_sem=pair_recv.at[step, lane],
                device_id={"sub": partner},
                device_id_type=MESH,
            )
            copy.start()
            pairs[step, lane] = copy

    def one(lane):
        value = p_ref[dev_at(at + lane, n), sub].astype(jnp.float32)
        for step in range(s - 1):
            pairs[step, lane].wait_recv()
            value = value + near[step, lane].astype(jnp.float32)
        return value

    def part(away, devs):
        front = one(away)
        if away == 0 or 2 * away == n:
            return (front, front)
        return (front, one(n - away))

    sent = ring_reduce(n, part, rows // 2, here, there, send_sem, recv_sem, out_ref)
    for copy in sent + list(pairs.values()):
        copy.wait_send()


def combine(n, s, parts, collective_id):
    _, _, rows, width = parts.shape
    sems = pltpu.SemaphoreType.DMA((2, 2, n // 2))
    pair = pltpu.SemaphoreType.DMA((max(s - 1, 1), n))
    return pl.pallas_call(
        functools.partial(combine_kernel, n, s),
        out_shape=jax.ShapeDtypeStruct((rows, width), jnp.float32),
        in_specs=[VMEM],
        out_specs=VMEM,
        scratch_shapes=[
            pltpu.VMEM((max(s - 1, 1), n, rows, width), jnp.bfloat16),
            pltpu.VMEM((2, 2, n // 2, rows // 2, width), jnp.bfloat16),
            pltpu.VMEM((2, 2, n // 2, rows // 2, width), jnp.bfloat16),
            sems,
            sems,
            pair,
            pair,
        ],
        compiler_params=pltpu.CompilerParams(collective_id=collective_id, has_side_effects=True),
        name="combine",
    )(parts)


def on_device(
    n,
    s,
    hidden,
    lengths,
    key_cache,
    value_cache,
    expert_ids,
    gate_codes,
    expert_device,
    attention_gain,
    mixture_gain,
    query_gain,
    key_gain,
    project_weight,
    output_weight,
    expert_gate_up,
    expert_down,
):
    rows, width = hidden.shape
    normed = norm_scale(hidden.astype(jnp.float32), attention_gain).astype(jnp.bfloat16)
    merged = project(n, normed, project_weight, 0)
    merged = merged.transpose(1, 0, 2).reshape(rows, -1)
    position = lengths.reshape(rows)
    split = HEADS * HD
    new = split + KVH * HD
    queries = merged[:, :split].astype(jnp.float32).reshape(rows, HEADS, HD)
    queries = rotate(norm_scale(queries, query_gain), position).astype(jnp.bfloat16)
    new_keys = merged[:, split:new].astype(jnp.float32).reshape(rows, KVH, HD)
    new_keys = rotate(norm_scale(new_keys, key_gain), position).astype(jnp.bfloat16)
    new_values = merged[:, new:].reshape(rows, KVH, HD)
    attention = attend(queries, new_keys, new_values, key_cache, value_cache, position)
    depth = output_weight.shape[0]
    projected = output(n, attention.reshape(rows, n, depth).transpose(1, 0, 2), output_weight, 1)
    residual = hidden.astype(jnp.float32) + projected
    mixture_in = norm_scale(residual, mixture_gain).astype(jnp.bfloat16)

    experts = expert_device.shape[0]
    numbers = jnp.arange(experts, dtype=jnp.int32)
    at_slot = (expert_device[:, None] == numbers[None, :])[None, None]
    named = (expert_ids[:, :, None] == numbers[None, None, :])[..., None]
    codes = jnp.sum(jnp.where(named & at_slot, gate_codes[:, :, None, None], 0), axis=(1, 2))
    coded = jnp.concatenate([codes // 32, codes % 32], axis=1).astype(jnp.bfloat16)
    extra = -(-coded.shape[1] // 128) * 128
    coded = jnp.pad(coded, ((0, 0), (0, extra - coded.shape[1])))
    everyone = gather(n, s, jnp.concatenate([mixture_in, coded], axis=1), 2)
    flat = everyone.reshape(n * s * rows, width + extra)
    arrived = flat[:, :width]
    tail = flat[:, width:].astype(jnp.float32)
    all_codes = tail[:, :experts] * 32.0 + tail[:, experts : 2 * experts]
    slot = lax.axis_index("dev") * s + lax.axis_index("sub")
    mine = jnp.sum(jnp.where(numbers[None, :] == slot, all_codes, 0.0), axis=1, keepdims=True)
    share = mine / jnp.sum(all_codes, axis=1, keepdims=True)
    both_parts = jnp.dot(arrived, expert_gate_up[0], preferred_element_type=jnp.float32)
    inner = expert_down.shape[1]
    units = (jax.nn.silu(both_parts[:, :inner]) * both_parts[:, inner:]).astype(jnp.bfloat16)
    result = jnp.dot(units, expert_down[0], preferred_element_type=jnp.float32).astype(jnp.bfloat16)
    parts = jnp.where(mine > 0.0, result.astype(jnp.float32) * share, 0.0).astype(jnp.bfloat16)
    routed = combine(n, s, parts.reshape(n, s, rows, width), 3)
    return (residual + routed).astype(jnp.bfloat16)


def solution(mesh):
    return jax.shard_map(
        functools.partial(on_device, mesh.shape["dev"], mesh.shape["sub"]),
        mesh=mesh,
        in_specs=(
            P(("groups", "dev", "sub"), None),
            P(("groups", "dev", "sub"), None),
            P(("groups", "dev", "sub"), None, None),
            P(("groups", "dev", "sub"), None, None),
            P(("groups", "dev", "sub"), None),
            P(("groups", "dev", "sub"), None),
            P(),
            P(),
            P(),
            P(),
            P(),
            P(None, "dev"),
            P("dev", None),
            P(("dev", "sub"), None, None),
            P(("dev", "sub"), None, None),
        ),
        out_specs=P(("groups", "dev", "sub"), None),
        check_vma=False,
    )
```

```python
import functools
import math

import jax
import jax.numpy as jnp
import numpy as np
from jax import lax
from jax.experimental import pallas as pl
from jax.experimental.pallas import tpu as pltpu
from jax.sharding import PartitionSpec as P

HEADS = 32
KVH = 4
HD = 128

EPSILON = 1e-06
ROPE_BASE = 1000000.0
MESH = pl.DeviceIdType.MESH
VMEM = pl.BlockSpec(memory_space=pltpu.VMEM)
ANY = pl.BlockSpec(memory_space=pl.ANY)


def norm_scale(values, scale_gain):
    mean_square = jnp.mean(values * values, axis=-1, keepdims=True)
    return values * lax.rsqrt(mean_square + EPSILON) * scale_gain


def place_of(dev, n):
    side = lax.rem(dev, 2)
    z = lax.div(dev, 2)
    return (1 - side) * z + side * (n - 1 - z)


def dev_at(place, n):
    place = lax.rem(place + 2 * n, n)
    side = lax.div(place, n // 2)
    return (1 - side) * (2 * place) + side * (2 * (n - 1 - place) + 1)


def greet(devs, subs=()):
    barrier = pltpu.get_barrier_semaphore()
    for dev in devs:
        pl.semaphore_signal(barrier, inc=1, device_id={"dev": dev}, device_id_type=MESH)
    for sub in subs:
        pl.semaphore_signal(barrier, inc=1, device_id={"sub": sub}, device_id_type=MESH)


def meet(count):
    pl.semaphore_wait(pltpu.get_barrier_semaphore(), count)


def reach(n, way, half):
    return n // 2 if way == half else n // 2 - 1


def ring_gather(n, x_ref, slot, send_sem, recv_sem, on_block, on_half=None):
    me = lax.axis_index("dev")
    at = place_of(me, n)
    rows = x_ref.shape[0] // 2
    sides = (dev_at(at + 1, n), dev_at(at - 1, n))
    sent = []

    def send(src, origin, way, half, hop):
        copy = pltpu.make_async_remote_copy(
            src_ref=src,
            dst_ref=slot(origin, half),
            send_sem=send_sem.at[way, half, hop],
            recv_sem=recv_sem.at[way, half, hop],
            device_id={"dev": sides[way]},
            device_id_type=MESH,
        )
        copy.start()
        sent.append(copy)

    for half in range(2):
        for way in range(2):
            if reach(n, way, half) >= 1:
                send(x_ref.at[pl.ds(half * rows, rows)], me, way, half, 0)
    on_block(0, (me,))
    for hop in range(1, n // 2 + 1):
        origins = (dev_at(at - hop, n), dev_at(at + hop, n))
        for half in range(2):
            for way in range(2):
                if hop > reach(n, way, half):
                    continue
                origin = origins[way]
                here = slot(origin, half)
                pltpu.make_async_remote_copy(
                    src_ref=here,
                    dst_ref=here,
                    send_sem=send_sem.at[way, half, hop - 1],
                    recv_sem=recv_sem.at[way, half, hop - 1],
                    device_id={"dev": sides[way]},
                    device_id_type=MESH,
                ).wait_recv()
                if hop < reach(n, way, half):
                    send(here, origin, way, half, hop)
                if on_half is not None:
                    on_half(origin, half)
        on_block(hop, origins[:1] if 2 * hop == n else origins)
    return sent


def ring_reduce(n, part, rows, here, there, send_sem, recv_sem, finish):
    at = place_of(lax.axis_index("dev"), n)
    sides = (dev_at(at + 1, n), dev_at(at - 1, n))
    sent = []
    for away in range(n // 2, -1, -1):
        both = part(away, (dev_at(at + away, n), dev_at(at - away, n)))
        for half in range(2):
            total = both[0][half * rows : (half + 1) * rows] if away == 0 else None
            for way in range(2):
                far = reach(n, way, half)
                if away > far:
                    continue
                value = total if away == 0 else both[way][half * rows : (half + 1) * rows]
                if away < far:
                    pltpu.make_async_remote_copy(
                        src_ref=there.at[way, half, away],
                        dst_ref=there.at[way, half, away],
                        send_sem=send_sem.at[way, half, away],
                        recv_sem=recv_sem.at[way, half, away],
                        device_id={"dev": sides[way]},
                        device_id_type=MESH,
                    ).wait_recv()
                    value = value + there[way, half, away].astype(jnp.float32)
                if away == 0:
                    total = value
                    continue
                here[way, half, away - 1] = value.astype(here.dtype)
                copy = pltpu.make_async_remote_copy(
                    src_ref=here.at[way, half, away - 1],
                    dst_ref=there.at[way, half, away - 1],
                    send_sem=send_sem.at[way, half, away - 1],
                    recv_sem=recv_sem.at[way, half, away - 1],
                    device_id={"dev": sides[way]},
                    device_id_type=MESH,
                )
                copy.start()
                sent.append(copy)
            if away == 0:
                finish(half, total)
    return sent


def others(n):
    me = lax.axis_index("dev")
    return [lax.rem(me + step, n) for step in range(1, n)]


def project_kernel(
    n, hidden_ref, gain_ref, rate_ref, length_ref, id_ref, code_ref, place_ref, w_hbm,
    out_ref, turn_ref, span_ref, coded_ref,
    x_ref, w_ref, held, mine, back, w_sem, send_sem, recv_sem, back_send, back_recv,
):
    me = lax.axis_index("dev")
    at = place_of(me, n)
    rows = x_ref.shape[0]
    half_rows = rows // 2
    load = pltpu.make_async_copy(w_hbm, w_ref, w_sem)
    load.start()
    greet(others(n))
    x_ref[...] = norm_scale(hidden_ref[...].astype(jnp.float32), gain_ref[...]).astype(x_ref.dtype)
    meet(n - 1)
    waiting = []
    returned = []

    def post():
        for dev, lane in waiting:
            copy = pltpu.make_async_remote_copy(
                src_ref=mine.at[lane],
                dst_ref=back.at[lane],
                send_sem=back_send.at[lane],
                recv_sem=back_recv.at[lane],
                device_id={"dev": dev},
                device_id_type=MESH,
            )
            copy.start()
            returned.append(copy)
        waiting.clear()

    def tables():
        across = lax.broadcasted_iota(jnp.int32, (rows, rows), 1)
        down = lax.broadcasted_iota(jnp.int32, (rows, rows), 0)
        lengths = jnp.broadcast_to(length_ref[...], (rows, rows))
        own = jnp.sum(jnp.where(across == down, lengths, 0), axis=1, keepdims=True)
        first = jnp.sum(jnp.where(across < down, lengths, 0), axis=1, keepdims=True)
        lanes = span_ref.shape[2]
        span_ref[0] = jnp.broadcast_to(first, (rows, lanes))
        span_ref[1] = jnp.broadcast_to(first + own, (rows, lanes))
        angles = own.astype(jnp.float32) * rate_ref[...]
        turn_ref[0] = jnp.cos(angles)
        side = lax.broadcasted_iota(jnp.int32, angles.shape, 1)
        sine = jnp.sin(angles)
        turn_ref[1] = jnp.where(side < lanes // 2, -sine, sine)
        experts = place_ref.shape[1]
        number = lax.broadcasted_iota(jnp.int32, (rows, experts), 1)
        lane = lax.broadcasted_iota(jnp.int32, (rows, coded_ref.shape[1]), 1)
        coded = jnp.zeros(lane.shape, jnp.int32)
        for choice in range(id_ref.shape[1]):
            named = number == id_ref[:, choice : choice + 1]
            holder = jnp.sum(jnp.where(named, place_ref[...], 0), axis=1, keepdims=True)
            code = code_ref[:, choice : choice + 1]
            coded = coded + jnp.where(lane == holder, code >> 5, 0)
            coded = coded + jnp.where(lane == holder + experts, code & 31, 0)
        coded_ref[...] = coded.astype(jnp.float32).astype(coded_ref.dtype)

    def on_block(hop, devs):
        if hop == 0:
            tables()
            load.wait()
            block = x_ref[...]
        else:
            block = jnp.concatenate([held[dev] for dev in devs], axis=0)
        product = jnp.dot(block, w_ref[...], preferred_element_type=jnp.float32).astype(mine.dtype)
        post()
        for index, dev in enumerate(devs):
            lane = hop if index == 0 else n - hop
            mine[lane] = product[index * rows : (index + 1) * rows]
            if hop > 0:
                waiting.append((dev, lane))

    sent = ring_gather(
        n,
        x_ref,
        lambda dev, half: held.at[dev, pl.ds(half * half_rows, half_rows)],
        send_sem,
        recv_sem,
        on_block,
    )
    post()
    out_ref[me] = mine[0]
    for copy in returned:
        copy.wait_recv()
    for lane in range(1, n):
        out_ref[dev_at(at + lane, n)] = back[lane]
    for copy in sent + returned:
        copy.wait_send()


def project(n, hidden, gain, lengths, ids, codes, places, w, collective_id):
    rows, width = hidden.shape
    columns = w.shape[1]
    sems = pltpu.SemaphoreType.DMA((2, 2, n // 2))
    lanes = pltpu.SemaphoreType.DMA((n,))
    rates = ROPE_BASE ** (-np.arange(HD // 2) * 2.0 / HD)
    rates = jnp.asarray(np.concatenate([rates, rates])[None, :], jnp.float32)
    extra = -(-2 * places.shape[0] // 128) * 128
    return pl.pallas_call(
        functools.partial(project_kernel, n),
        out_shape=(
            jax.ShapeDtypeStruct((n, rows, columns), jnp.bfloat16),
            jax.ShapeDtypeStruct((2, rows, HD), jnp.float32),
            jax.ShapeDtypeStruct((2, rows, HD), jnp.int32),
            jax.ShapeDtypeStruct((rows, extra), jnp.bfloat16),
        ),
        in_specs=[VMEM] * 7 + [ANY],
        out_specs=[VMEM] * 4,
        scratch_shapes=[
            pltpu.VMEM((rows, width), jnp.bfloat16),
            pltpu.VMEM(w.shape, w.dtype),
            pltpu.VMEM((n, rows, width), jnp.bfloat16),
            pltpu.VMEM((n, rows, columns), jnp.bfloat16),
            pltpu.VMEM((n, rows, columns), jnp.bfloat16),
            pltpu.SemaphoreType.DMA,
            sems,
            sems,
            lanes,
            lanes,
        ],
        compiler_params=pltpu.CompilerParams(collective_id=collective_id, has_side_effects=True),
        name="project",
    )(hidden, gain[None, :], rates, lengths, ids, codes, places[None, :], w)


def attend_kernel(
    tile, merged_ref, turn_ref, span_ref, query_gain_ref, key_gain_ref, k_hbm, v_hbm,
    out_ref, k_ref, v_ref, kept, k_sem, v_sem,
):
    width = HD
    loads = []
    for head in range(KVH):
        columns = pl.ds(head * width, width)
        for source, target, sem in ((k_hbm, k_ref, k_sem), (v_hbm, v_ref, v_sem)):
            copy = pltpu.make_async_copy(source.at[0, :, columns], target.at[head], sem.at[head])
            copy.start()
            loads.append(copy)
    rows = merged_ref.shape[1]
    scale = 1.0 / math.sqrt(width)
    fan = HEADS // KVH
    lines = rows * fan
    per_in = merged_ref.shape[2]
    per_out = out_ref.shape[2]

    def columns_of(head):
        pieces = []
        low, high = head * width, (head + 1) * width
        while low < high:
            dev, start = low // per_in, low % per_in
            count = min(high - low, per_in - start)
            pieces.append(merged_ref[dev, :, start : start + count].astype(jnp.float32))
            low += count
        return pieces[0] if len(pieces) == 1 else jnp.concatenate(pieces, axis=1)

    def turned(head, gain):
        values = norm_scale(columns_of(head), gain)
        swapped = jnp.concatenate([values[:, width // 2 :], values[:, : width // 2]], axis=1)
        return (values * turn_ref[0] + swapped * turn_ref[1]).astype(jnp.bfloat16)

    repeat = lambda values: jnp.concatenate([values] * fan, axis=0)
    first = repeat(span_ref[0][:, :1])
    last = repeat(span_ref[1][:, :1])
    tiles = k_ref.shape[1] // tile
    lane = lax.broadcasted_iota(jnp.int32, (1, tile), 1)
    for head in range(KVH):
        queries = [turned(head * fan + g, query_gain_ref[...]) for g in range(fan)]
        new_key = turned(HEADS + head, key_gain_ref[...]).astype(jnp.float32)
        new_value = repeat(columns_of(HEADS + KVH + head))
        q = jnp.concatenate(queries, axis=0)
        own = jnp.concatenate(
            [jnp.sum(one.astype(jnp.float32) * new_key, axis=1, keepdims=True) for one in queries], axis=0
        )
        peak = own
        loads[2 * head].wait()
        for index in range(tiles):
            keys = k_ref[head, index * tile : (index + 1) * tile]
            score = lax.dot_general(q, keys, (((1,), (1,)), ((), ())), preferred_element_type=jnp.float32)
            position = lane + index * tile
            inside = (position >= first) & (position < last)
            score = jnp.where(inside, score, -1e30)
            kept[index] = score
            peak = jnp.maximum(peak, jnp.max(score, axis=1, keepdims=True))
        own_raised = jnp.exp((own - peak) * scale)
        total = own_raised
        mixed = own_raised * new_value
        loads[2 * head + 1].wait()
        for index in range(tiles):
            raised = jnp.exp((kept[index] - peak) * scale)
            total = total + jnp.sum(raised, axis=1, keepdims=True)
            mixed = mixed + jnp.dot(
                raised.astype(jnp.bfloat16),
                v_ref[head, index * tile : (index + 1) * tile],
                preferred_element_type=jnp.float32,
            )
        result = (mixed / total).astype(out_ref.dtype)
        for g in range(fan):
            start = (head * fan + g) * width
            out_ref[start // per_out, :, start % per_out : start % per_out + width] = result[g * rows : (g + 1) * rows]


def attend(n, merged, turns, spans, query_gain, key_gain, key_cache, value_cache):
    rows = merged.shape[1]
    pool = key_cache.shape[1]
    tile = math.gcd(pool, 1024)
    return pl.pallas_call(
        functools.partial(attend_kernel, tile),
        out_shape=jax.ShapeDtypeStruct((n, rows, HEADS * HD // n), jnp.bfloat16),
        in_specs=[VMEM] * 5 + [ANY] * 2,
        out_specs=VMEM,
        scratch_shapes=[
            pltpu.VMEM((KVH, pool, HD), jnp.bfloat16),
            pltpu.VMEM((KVH, pool, HD), jnp.bfloat16),
            pltpu.VMEM((pool // tile, rows * HEADS // KVH, tile), jnp.float32),
            pltpu.SemaphoreType.DMA((KVH,)),
            pltpu.SemaphoreType.DMA((KVH,)),
        ],
        name="attend",
    )(merged, turns, spans, query_gain[None, :], key_gain[None, :], key_cache, value_cache)


def others(n):
    me = lax.axis_index("dev")
    return [lax.rem(me + step, n) for step in range(1, n)]


def tail_kernel(
    n, s, experts, a_ref, hidden_ref, gain_ref, coded_ref, w_hbm, up_hbm, down_hbm, out_ref,
    w_ref, up_ref, down_ref, load_sem, held, here, there, residual, x_ref, every, units, parts, near,
    sum_send, sum_recv, move_send, move_recv, ring_send, ring_recv, pair_send, pair_recv,
    near_send, near_recv, home_send, home_recv, back_here, back_there,
):
    me = lax.axis_index("dev")
    at = place_of(me, n)
    sub = lax.axis_index("sub")
    rows = a_ref.shape[1]
    half_rows = rows // 2
    width = hidden_ref.shape[1]
    loads = []
    for index, (source, target) in enumerate(((w_hbm, w_ref), (up_hbm.at[0], up_ref), (down_hbm.at[0], down_ref))):
        copy = pltpu.make_async_copy(source, target, load_sem.at[index])
        copy.start()
        loads.append(copy)
    partners = [lax.rem(sub + step, s) for step in range(1, s)]
    greet(others(n), partners)
    meet(n - 1 + s - 1)

    moves = {}
    order = [n // 2]
    for away in range(n // 2 - 1, 0, -1):
        order += [away, n - away]
    for lane in order:
        copy = pltpu.make_async_remote_copy(
            src_ref=a_ref.at[dev_at(at - lane, n)],
            dst_ref=held.at[lane],
            send_sem=move_send.at[lane],
            recv_sem=move_recv.at[lane],
            device_id={"dev": dev_at(at - lane, n)},
            device_id_type=MESH,
        )
        copy.start()
        moves[lane] = copy
    loads[0].wait()

    def projected(away, devs):
        lanes = (away,) if away == 0 or 2 * away == n else (away, n - away)
        if away == 0:
            features = a_ref[me]
        else:
            for lane in lanes:
                moves[lane].wait_recv()
            features = jnp.concatenate([held[lane] for lane in lanes], axis=0)
        product = jnp.dot(features, w_ref[...], preferred_element_type=jnp.float32)
        return (product[:rows], product[-rows:])

    def normed(half, total):
        chosen = pl.ds(half * half_rows, half_rows)
        value = hidden_ref[chosen, :].astype(jnp.float32) + total
        residual[chosen, :] = value
        x_ref[chosen, :width] = norm_scale(value, gain_ref[...]).astype(x_ref.dtype)
        x_ref[chosen, width:] = coded_ref[chosen, :]

    sent = ring_reduce(n, projected, half_rows, here, there, sum_send, sum_recv, normed)
    for copy in moves.values():
        copy.wait_send()

    pairs = {}

    def share(src, origin, key, half):
        for step, partner in enumerate(partners):
            copy = pltpu.make_async_remote_copy(
                src_ref=src,
                dst_ref=every.at[origin, sub, pl.ds(half * half_rows, half_rows)],
                send_sem=pair_send.at[step, origin, half],
                recv_sem=pair_recv.at[step, origin, half],
                device_id={"sub": partner},
                device_id_type=MESH,
            )
            copy.start()
            sent.append(copy)

    slot = lambda dev, half: every.at[dev, sub, pl.ds(half * half_rows, half_rows)]
    number = me * s + sub
    inner = down_ref.shape[0]
    tile = math.gcd(inner, 256)
    block = s * rows

    def expert(hop, devs):
        if hop == 0:
            for half in range(2):
                share(x_ref.at[pl.ds(half * half_rows, half_rows)], me, None, half)
            every[me, sub] = x_ref[...]
            for copy in loads[1:]:
                copy.wait()
        for dev in devs:
            for half in range(2):
                for step, partner in enumerate(partners):
                    came = every.at[dev, lax.rem(sub + s - step - 1, s), pl.ds(half * half_rows, half_rows)]
                    pltpu.make_async_remote_copy(
                        src_ref=came,
                        dst_ref=came,
                        send_sem=pair_send.at[step, dev, half],
                        recv_sem=pair_recv.at[step, dev, half],
                        device_id={"sub": partner},
                        device_id_type=MESH,
                    ).wait_recv()
        count = block * len(devs)
        whole = jnp.concatenate([every[dev].reshape(block, every.shape[3]) for dev in devs], axis=0)
        inputs = whole[:, :width]
        codes = whole[:, width:].astype(jnp.float32)
        lane = lax.broadcasted_iota(jnp.int32, codes.shape, 1)
        high = jnp.where(lane < experts, 32.0, jnp.where(lane < 2 * experts, 1.0, 0.0))
        worth = codes * high
        total = jnp.sum(worth, axis=1, keepdims=True)
        mine = jnp.where((lane == number) | (lane == number + experts), worth, 0.0)
        mine = jnp.sum(mine, axis=1, keepdims=True)
        weight = mine / total
        for start in range(0, inner, tile):
            gate = jnp.dot(inputs, up_ref[:, start : start + tile], preferred_element_type=jnp.float32)
            up = jnp.dot(inputs, up_ref[:, inner + start : inner + start + tile], preferred_element_type=jnp.float32)
            units[:count, start : start + tile] = (gate / (1.0 + jnp.exp(-gate)) * up).astype(units.dtype)
        result = jnp.dot(units[:count, :], down_ref[...], preferred_element_type=jnp.float32)
        result = result.astype(jnp.bfloat16).astype(jnp.float32)
        result = jnp.where(mine > 0.0, result * weight, 0.0).astype(parts.dtype)
        for index, dev in enumerate(devs):
            parts[dev] = result[index * block : (index + 1) * block].reshape(s, rows, width)
        for dev in devs:
            for step, partner in enumerate(partners):
                copy = pltpu.make_async_remote_copy(
                    src_ref=parts.at[dev, partner],
                    dst_ref=near.at[step, dev],
                    send_sem=near_send.at[step, dev],
                    recv_sem=near_recv.at[step, dev],
                    device_id={"sub": partner},
                    device_id_type=MESH,
                )
                copy.start()
                sent.append(copy)

    sent += ring_gather(
        n, x_ref, slot, ring_send, ring_recv, expert, lambda dev, half: share(slot(dev, half), dev, None, half)
    )

    def one(dev):
        value = parts[dev, sub].astype(jnp.float32)
        for step, partner in enumerate(partners):
            pltpu.make_async_remote_copy(
                src_ref=near.at[step, dev],
                dst_ref=near.at[step, dev],
                send_sem=near_send.at[step, dev],
                recv_sem=near_recv.at[step, dev],
                device_id={"sub": partner},
                device_id_type=MESH,
            ).wait_recv()
            value = value + near[step, dev].astype(jnp.float32)
        return value

    def routed(away, devs):
        front = one(devs[0])
        if away == 0 or 2 * away == n:
            return (front, front)
        return (front, one(devs[1]))

    def finish(half, total):
        chosen = pl.ds(half * half_rows, half_rows)
        out_ref[chosen, :] = (residual[chosen, :] + total).astype(out_ref.dtype)

    sent += ring_reduce(n, routed, half_rows, back_here, back_there, home_send, home_recv, finish)
    for copy in sent:
        copy.wait_send()


def tail(n, s, experts, a, hidden, gain, coded, w, up, down, collective_id):
    rows, width = hidden.shape
    extra = coded.shape[1]
    ring = pltpu.SemaphoreType.DMA((2, 2, n // 2))
    lanes = pltpu.SemaphoreType.DMA((n,))
    pair = pltpu.SemaphoreType.DMA((max(s - 1, 1), n, 2))
    near = pltpu.SemaphoreType.DMA((max(s - 1, 1), n))
    sums = pltpu.VMEM((2, 2, n // 2, rows // 2, width), jnp.bfloat16)
    return pl.pallas_call(
        functools.partial(tail_kernel, n, s, experts),
        out_shape=jax.ShapeDtypeStruct((rows, width), jnp.bfloat16),
        in_specs=[VMEM] * 4 + [ANY] * 3,
        out_specs=VMEM,
        scratch_shapes=[
            pltpu.VMEM(w.shape, w.dtype),
            pltpu.VMEM(up.shape[1:], up.dtype),
            pltpu.VMEM(down.shape[1:], down.dtype),
            pltpu.SemaphoreType.DMA((3,)),
            pltpu.VMEM((n,) + a.shape[1:], a.dtype),
            sums,
            sums,
            pltpu.VMEM((rows, width), jnp.float32),
            pltpu.VMEM((rows, width + extra), jnp.bfloat16),
            pltpu.VMEM((n, s, rows, width + extra), jnp.bfloat16),
            pltpu.VMEM((2 * s * rows, down.shape[1]), jnp.bfloat16),
            pltpu.VMEM((n, s, rows, width), jnp.bfloat16),
            pltpu.VMEM((max(s - 1, 1), n, rows, width), jnp.bfloat16),
            ring, ring, lanes, lanes, ring, ring, pair, pair, near, near, ring, ring, sums, sums,
        ],
        compiler_params=pltpu.CompilerParams(collective_id=collective_id, has_side_effects=True),
        name="tail",
    )(a, hidden, gain[None, :], coded, w, up, down)


def on_device(
    n,
    s,
    hidden,
    lengths,
    key_cache,
    value_cache,
    expert_ids,
    gate_codes,
    expert_device,
    attention_gain,
    mixture_gain,
    query_gain,
    key_gain,
    project_weight,
    output_weight,
    expert_gate_up,
    expert_down,
):
    merged, turns, spans, coded = project(
        n, hidden, attention_gain, lengths, expert_ids, gate_codes, expert_device, project_weight, 0
    )
    attention = attend(n, merged, turns, spans, query_gain, key_gain, key_cache, value_cache)
    experts = expert_device.shape[0]
    return tail(
        n, s, experts, attention, hidden, mixture_gain, coded, output_weight, expert_gate_up, expert_down, 1
    )


def solution(mesh):
    return jax.shard_map(
        functools.partial(on_device, mesh.shape["dev"], mesh.shape["sub"]),
        mesh=mesh,
        in_specs=(
            P(("groups", "dev", "sub"), None),
            P(("groups", "dev", "sub"), None),
            P(("groups", "dev", "sub"), None, None),
            P(("groups", "dev", "sub"), None, None),
            P(("groups", "dev", "sub"), None),
            P(("groups", "dev", "sub"), None),
            P(),
            P(),
            P(),
            P(),
            P(),
            P(None, "dev"),
            P("dev", None),
            P(("dev", "sub"), None, None),
            P(("dev", "sub"), None, None),
        ),
        out_specs=P(("groups", "dev", "sub"), None),
        check_vma=False,
    )
```
